32 devices in a mesh: gx: 4 (over y, x), gy: 4 (over z), gz: 2 (over core).
Axes of the slice: x: 2, y: 2, z: 4, core: 2. Of those that a mesh axis runs over, the one named last changes fastest.
Arguments:
- populations: float32 [19, 8, 64, 256], P(None, 'gx', 'gy', 'gz'), may hold values from 0.005 to 0.8, as said below
- porosity: float32 [8, 64, 256], P('gx', 'gy', 'gz'), may hold values from 0.05 to 0.45
- solid: int32 [8, 64, 256], P('gx', 'gy', 'gz'), may hold values 0 or 1
- seed_adjoint: float32 [19, 8, 64, 256], P(None, 'gx', 'gy', 'gz'), may hold values from -60 to 60
Outputs:
- porosity_grad: float32 [8, 64, 256], P('gx', 'gy', 'gz')
- initial_adjoint: float32 [19, 8, 64, 256], P(None, 'gx', 'gy', 'gz')
The draws below stay inside these ranges and needn't reach their ends.
Inputs may be any that keep to these rules, and one draw needn't show every extreme that they name: `populations`: every population is positive.
All inputs are finite; a program needn't handle non-finite values. No bound on the sum of `solid` on one device may be relied on, other than what follows from the above.
Results may differ from the reference program's by a relative error of at most 0.0003.
Values sent between devices are 32-bit elements; how exact they have to be, the bound alone decides.
A program may use at most 64 MiB of HBM per device.

```python
import jax
import jax.numpy as jnp
from jax import lax

Q = 19
STEPS = 3
NX = 8
NY = 64
NZ = 256


LATTICE_WEIGHTS = [1.0 / 3.0] + [1.0 / 18.0] * 6 + [1.0 / 36.0] * 12


def draw_populations(key, part):
    key_density = jax.random.fold_in(key, 11)
    key_jitter = jax.random.fold_in(key, 12)
    weight_table = jnp.asarray(LATTICE_WEIGHTS, jnp.float32).reshape(19, 1, 1, 1)
    density = jax.random.uniform(key_density, (NX, NY, NZ), jnp.float32, 0.7, 1.4)
    jitter = jax.random.uniform(key_jitter, (19, NX, NY, NZ), jnp.float32, -0.35, 0.35)
    factor = 1.0 + jitter
    return weight_table * density * factor


def with_ends(entries, rng, least, high):
    longest = entries.shape.index(max(entries.shape))
    spots = []
    for shift in (0, 1):
        where = [jax.random.randint(jax.random.fold_in(rng, axis), (), 0, length) for axis, length in enumerate(entries.shape)]
        where[longest] = (where[longest] + shift) % entries.shape[longest]
        spots.append(tuple(where))
    return entries.at[spots[0]].set(least).at[spots[1]].set(high)


def block_scale(own_key, dims, cuts, low, largest):
    loudness = 1.0
    for axis_at, blocks in cuts:
        heights = jax.random.uniform(jax.random.fold_in(jax.random.fold_in(own_key, 6), axis_at), (blocks,), jnp.float32, low / len(cuts), largest / len(cuts))
        loudness = loudness * jnp.repeat(jnp.exp(heights), dims[axis_at] // blocks).reshape((-1,) + (1,) * (len(dims) - 1 - axis_at))
    return loudness


def normal_values(own_key, dims, deviation, limit, split=(), kind=jnp.bfloat16):
    array = jax.random.normal(own_key, dims, jnp.float32) * deviation
    if len(split) > 0:
        array = block_scale(own_key, dims, split, -0.22, 0.18) * array
    return jnp.clip(array, min=-limit, max=limit).astype(kind)


def setup_inputs(seed: int = 0) -> dict:
    seeds = jax.random.split(jax.random.key(seed), 5)
    populations = draw_populations(jax.random.fold_in(seeds[4], 71), 0)
    porosity = jnp.clip(0.05 + 0.39999999 * jax.random.uniform(seeds[1], (NX, NY, NZ), jnp.float32) ** block_scale(seeds[1], (NX, NY, NZ), ((0, 4), (1, 4), (2, 2)), -0.2, 0.2), 0.05, 0.45)
    solid = with_ends((jax.random.randint(seeds[2], (NX, NY, NZ), 0, 8) < 1).astype(jnp.int32), jax.random.fold_in(seeds[2], 1), 0, 1)
    seed_adjoint = normal_values(seeds[3], (Q, NX, NY, NZ), 10.0, 60.0, ((1, 4), (2, 4), (3, 2)), jnp.float32)
    return {"populations": populations, "porosity": porosity, "solid": solid, "seed_adjoint": seed_adjoint}


VELOCITIES = [[0, 0, 0], [1, 0, 0], [-1, 0, 0], [0, 1, 0], [0, -1, 0], [0, 0, 1], [0, 0, -1], [1, 1, 0], [-1, -1, 0], [1, -1, 0], [-1, 1, 0], [1, 0, 1], [-1, 0, -1], [1, 0, -1], [-1, 0, 1], [0, 1, 1], [0, -1, -1], [0, 1, -1], [0, -1, 1]]
OPPOSITE = [0, 2, 1, 4, 3, 6, 5, 8, 7, 10, 9, 12, 11, 14, 13, 16, 15, 18, 17]
LATTICE_WEIGHTS = [1.0 / 3.0] + [1.0 / 18.0] * 6 + [1.0 / 36.0] * 12
OMEGA = 1.25

def relax_collision(field, porosity, solid):
    dtype = field.dtype
    vel_table = jnp.asarray(VELOCITIES, dtype=dtype)
    weight_table = jnp.asarray(LATTICE_WEIGHTS, dtype=dtype).reshape(19, 1, 1, 1)
    density = lax.optimization_barrier(jnp.sum(field, axis=0))
    momentum = jnp.tensordot(vel_table.T, field, axes=1, precision=lax.Precision.HIGHEST)
    velocity = momentum / density
    projected = jnp.tensordot(vel_table, velocity, axes=1, precision=lax.Precision.HIGHEST)
    speed_sq = lax.optimization_barrier(jnp.sum(velocity * velocity, axis=0))
    equilibrium = weight_table * density * (1.0 + 3.0 * projected + 4.5 * projected * projected - 1.5 * speed_sq)
    relaxed = field - OMEGA * (field - equilibrium)
    bounced = jnp.stack([field[index] for index in OPPOSITE])
    blocking = jnp.where(solid == 1, jnp.ones_like(porosity), porosity)
    return (1.0 - blocking) * relaxed + blocking * bounced

def translate(field, sign):
    return jnp.stack([jnp.roll(field[index], (sign * vel[0], sign * vel[1], sign * vel[2]), axis=(0, 1, 2)) for index, vel in enumerate(VELOCITIES)])

def reference(populations, porosity, solid, seed_adjoint):
    state_history = [populations]
    current = populations
    for lattice_update in range(STEPS):
        current = translate(relax_collision(current, porosity, solid), 1)
        state_history.append(current)
    adjoint = seed_adjoint
    gradient = jnp.zeros_like(porosity)
    for lattice_update in range(STEPS - 1, -1, -1):
        pulled = translate(adjoint, -1)
        unused_value, backward_pullback = jax.vjp(lambda flow_field, porosity_field: relax_collision(flow_field, porosity_field, solid), state_history[lattice_update], porosity)
        adjoint, grad_part = backward_pullback(pulled)
        gradient = gradient + grad_part
    return (gradient, adjoint)
```

```python
import functools

import jax
import jax.numpy as jnp
from jax import lax
from jax.experimental import pallas as pl
from jax.experimental.pallas import tpu as pltpu
from jax.sharding import PartitionSpec as P

STEPS = 3
STREAMS = 5
AXES = ("gx", "gy", "gz")
Q = 19

VEL = [
    (0, 0, 0),
    (1, 0, 0),
    (-1, 0, 0),
    (0, 1, 0),
    (0, -1, 0),
    (0, 0, 1),
    (0, 0, -1),
    (1, 1, 0),
    (-1, -1, 0),
    (1, -1, 0),
    (-1, 1, 0),
    (1, 0, 1),
    (-1, 0, -1),
    (1, 0, -1),
    (-1, 0, 1),
    (0, 1, 1),
    (0, -1, -1),
    (0, 1, -1),
    (0, -1, 1),
]
OPP = [0, 2, 1, 4, 3, 6, 5, 8, 7, 10, 9, 12, 11, 14, 13, 16, 15, 18, 17]
W = [1.0 / 3.0] + [1.0 / 18.0] * 6 + [1.0 / 36.0] * 12
OMEGA = 1.25
PAIRS = [(i, OPP[i]) for i in range(1, Q, 2)]

FACE = {
    m: [j for j in range(Q) if any(c and c == d for c, d in zip(VEL[j], VEL[m]))]
    for m in range(1, 7)
}
SEND_ORDER = [7, 8, 9, 10, 1, 2, 11, 12, 13, 14, 15, 16, 17, 18, 3, 4, 5, 6]


def face_of(axis, sign):
    return 1 + 2 * axis + (0 if sign > 0 else 1)


def signed(terms):
    total = None
    for sign, value in terms:
        if total is None:
            total = value if sign > 0 else -value
        else:
            total = total + value if sign > 0 else total - value
    return total


def moments(odd):
    return [
        signed([(VEL[i][d], odd[i]) for i, _ in PAIRS if VEL[i][d]]) for d in range(3)
    ]


def dot_c(vel, vec):
    return signed([(vel[d], vec[d]) for d in range(3) if vel[d]])


def flow(f):
    even = {i: f[i] + f[o] for i, o in PAIRS}
    odd = {i: f[i] - f[o] for i, o in PAIRS}
    rho = f[0]
    for i, _ in PAIRS:
        rho = rho + even[i]
    inv = 1.0 / rho
    u = [m * inv for m in moments(odd)]
    return even, odd, rho, u


def collide(f, block):
    even, odd, rho, u = flow(f)
    speed = u[0] * u[0] + u[1] * u[1] + u[2] * u[2]
    fluid = 1.0 - block
    keep_even = fluid * (1.0 - OMEGA) + block
    keep_odd = fluid * (1.0 - OMEGA) - block
    push = fluid * OMEGA * rho
    base = 1.0 - 1.5 * speed
    out = [None] * Q
    out[0] = keep_even * f[0] + push * W[0] * base
    half_even = 0.5 * keep_even
    half_odd = 0.5 * keep_odd
    weighted = {w: push * w for w in set(W[1:])}
    for i, o in PAIRS:
        p = dot_c(VEL[i], u)
        scale = weighted[W[i]]
        e = half_even * even[i] + scale * (base + 4.5 * (p * p))
        q = half_odd * odd[i] + scale * (3.0 * p)
        out[i] = e + q
        out[o] = e - q
    return out


def adjoint(f, b, block, open_cell):
    even, odd, rho, u = flow(f)
    speed = u[0] * u[0] + u[1] * u[1] + u[2] * u[2]
    beven = {i: b[i] + b[o] for i, o in PAIRS}
    bodd = {i: b[i] - b[o] for i, o in PAIRS}
    weven = {i: W[i] * beven[i] for i, _ in PAIRS}
    e0 = W[0] * b[0]
    for i, _ in PAIRS:
        e0 = e0 + weven[i]
    e1 = moments({i: W[i] * bodd[i] for i, _ in PAIRS})

    def second(d, k):
        return signed(
            [
                (VEL[i][d] * VEL[i][k], weven[i])
                for i, _ in PAIRS
                if VEL[i][d] * VEL[i][k]
            ]
        )

    q = [[None] * 3 for _ in range(3)]
    for d in range(3):
        for k in range(d, 3):
            q[d][k] = q[k][d] = second(d, k)
    qu = [q[d][0] * u[0] + q[d][1] * u[1] + q[d][2] * u[2] for d in range(3)]
    uqu = qu[0] * u[0] + qu[1] * u[1] + qu[2] * u[2]
    ue1 = e1[0] * u[0] + e1[1] * u[1] + e1[2] * u[2]
    tail = 4.5 * uqu - 1.5 * speed * e0
    b_feq = rho * (e0 + 3.0 * ue1 + tail)
    fluid = 1.0 - block
    push = fluid * OMEGA
    g0 = push * (e0 - tail)
    g = [push * (3.0 * e1[d] + 9.0 * qu[d] - 3.0 * (u[d] * e0)) for d in range(3)]
    se = None
    so = None
    for i, _ in PAIRS:
        x = beven[i] * even[i]
        y = bodd[i] * odd[i]
        se = x if se is None else se + x
        so = y if so is None else so + y
    rest = b[0] * f[0]
    b_f = rest + 0.5 * (se + so)
    b_fopp = rest + 0.5 * (se - so)
    grad = open_cell * (b_fopp - (1.0 - OMEGA) * b_f - OMEGA * b_feq)
    keep_even = fluid * (1.0 - OMEGA) + block
    half_even = 0.5 * keep_even
    half_odd = 0.5 * (fluid * (1.0 - OMEGA) - block)
    a = [None] * Q
    a[0] = keep_even * b[0] + g0
    for i, o in PAIRS:
        e = half_even * beven[i] + g0
        h = half_odd * bodd[i] + dot_c(VEL[i], g)
        a[i] = e + h
        a[o] = e - h
    return a, grad


def kernel(
    sizes,
    f_hbm,
    por_hbm,
    sol_hbm,
    a_hbm,
    grad_out,
    adj_out,
    f0,
    por,
    sol,
    a3,
    f1,
    bbuf,
    post,
    xs,
    xr,
    ys,
    yr,
    zs,
    zr,
    e1s,
    e1r,
    e2s,
    e2r,
    in_sem,
    send_sem,
    recv_sem,
):
    lx, ly, lz = por.shape
    here = [lax.axis_index(name) for name in AXES]

    def neighbour(vel):
        return tuple(
            lax.rem(here[d] + (vel[d] + sizes[d]), sizes[d]) if vel[d] else here[d]
            for d in range(3)
        )

    barrier = pltpu.get_barrier_semaphore()
    for m in SEND_ORDER:
        pl.semaphore_signal(
            barrier,
            inc=1,
            device_id=neighbour(VEL[m]),
            device_id_type=pl.DeviceIdType.MESH,
        )
    loads = [
        pltpu.make_async_copy(src, dst, in_sem.at[k])
        for k, (src, dst) in enumerate(
            [(f_hbm, f0), (por_hbm, por), (sol_hbm, sol), (a_hbm, a3)]
        )
    ]
    for load in loads:
        load.start()

    row = lax.broadcasted_iota(jnp.int32, (ly, lz), 0)
    lane = lax.broadcasted_iota(jnp.int32, (ly, lz), 1)
    lane1 = lax.broadcasted_iota(jnp.int32, (1, lz), 1)
    diagonal = row == lane

    def last(sign, n):
        return n - 1 if sign > 0 else 0

    def buffers(s, m, x, y, z, e1, e2):
        if m <= 2:
            return x.at[s, m - 1]
        if m <= 4:
            return y.at[s, m - 3]
        if m <= 6:
            return z.at[s, m - 5]
        if m <= 14:
            return e1.at[s, m - 7]
        return e2.at[s, m - 15]

    def copy_of(s, m):
        return pltpu.make_async_remote_copy(
            src_ref=buffers(s, m, xs, ys, zs, e1s, e2s),
            dst_ref=buffers(s, m, xr, yr, zr, e1r, e2r),
            send_sem=send_sem.at[s, m - 1],
            recv_sem=recv_sem.at[s, m - 1],
            device_id=neighbour(VEL[m]),
            device_id_type=pl.DeviceIdType.MESH,
        )

    def send(s):
        for m in SEND_ORDER:
            copy_of(s, m).start()

    def arrived(s):
        for m in SEND_ORDER:
            copy_of(s, m).wait_recv()

    def put(s, plane, values, packs):
        for j in range(Q):
            cx, cy, cz = VEL[j]
            v = values[j]
            leaves = cx != 0 and plane == last(cx, lx)
            if leaves:
                m = face_of(0, cx)
                xs[s, m - 1, FACE[m].index(j)] = v
                if cy:
                    r = last(cy, ly)
                    e1s[s, j - 7] = v[r : r + 1, :]
                if cz:
                    c = last(cz, lz)
                    column = jnp.broadcast_to(v[:, c : c + 1], (ly, lz))
                    e1s[s, j - 7] = jnp.sum(
                        jnp.where(diagonal, column, 0.0), axis=0, keepdims=True
                    )
            else:
                post[s, j, plane] = v
            if cy:
                m = face_of(1, cy)
                r = last(cy, ly)
                k = FACE[m].index(j) * lx + plane
                ys[s, m - 3, k : k + 1, :] = v[r : r + 1, :]
                if cz:
                    e2s[s, j - 15, plane : plane + 1, :] = v[r : r + 1, :]
            if cz:
                m = face_of(2, cz)
                k = FACE[m].index(j) * lx + plane
                turned = pltpu.roll(v, (k - last(cz, lz)) % lz, 1)
                old = packs.get(m)
                packs[m] = turned if old is None else jnp.where(lane == k, turned, old)

    def put_packs(s, packs):
        for m in (5, 6):
            zs[s, m - 5] = packs[m]

    def assemble(s, plane):
        packs = [zr[s, 0], zr[s, 1]]
        out = []
        for j in range(Q):
            cx, cy, cz = VEL[j]
            source = plane - cx
            inside = 0 <= source < lx
            if inside:
                v = post[s, j, source]
            else:
                m = face_of(0, cx)
                v = xr[s, m - 1, FACE[m].index(j)]
            if cz:
                c = last(cz, lz)
                if inside:
                    m = face_of(2, cz)
                    k = FACE[m].index(j) * lx + source
                    column = pltpu.roll(packs[m - 5], (c - k) % lz, 1)
                else:
                    line = jnp.broadcast_to(e1r[s, j - 7], (ly, lz))
                    column = jnp.sum(
                        jnp.where(diagonal, line, 0.0), axis=1, keepdims=True
                    )
                v = jnp.where(lane == c, column, v)
            if cy:
                r = last(cy, ly)
                if inside:
                    m = face_of(1, cy)
                    k = FACE[m].index(j) * lx + source
                    line = yr[s, m - 3, k : k + 1, :]
                    if cz:
                        line = jnp.where(
                            lane1 == last(cz, lz),
                            e2r[s, j - 15, source : source + 1, :],
                            line,
                        )
                else:
                    line = e1r[s, j - 7]
                v = jnp.where(row == r, jnp.broadcast_to(line, (ly, lz)), v)
                v = pltpu.roll(v, cy % ly, 0)
            if cz:
                v = pltpu.roll(v, cz % lz, 1)
            out.append(v)
        return out

    def blocking(plane):
        solid = sol[plane] == 1
        return jnp.where(solid, 1.0, por[plane]), jnp.where(solid, 0.0, 1.0)

    def flip(values):
        return [values[OPP[j]] for j in range(Q)]

    for load in loads[:3]:
        load.wait()
    packs = {}
    for plane in range(lx):
        block, _ = blocking(plane)
        put(0, plane, collide([f0[j, plane] for j in range(Q)], block), packs)
    put_packs(0, packs)
    pl.semaphore_wait(barrier, len(SEND_ORDER))
    send(0)

    loads[3].wait()
    packs = {}
    for plane in range(lx):
        put(2, plane, flip([a3[j, plane] for j in range(Q)]), packs)
    put_packs(2, packs)
    send(2)

    arrived(0)
    packs = {}
    for plane in range(lx):
        f = assemble(0, plane)
        for j in range(Q):
            f1[j, plane] = f[j]
        block, _ = blocking(plane)
        put(1, plane, collide(f, block), packs)
    put_packs(1, packs)
    send(1)

    arrived(2)
    for plane in range(lx):
        b = assemble(2, plane)
        for j in range(Q):
            bbuf[j, plane] = b[j]
    arrived(1)
    packs = {}
    for plane in range(lx):
        f = assemble(1, plane)
        b = flip([bbuf[j, plane] for j in range(Q)])
        a, grad = adjoint(f, b, *blocking(plane))
        grad_out[plane] = grad
        put(3, plane, flip(a), packs)
    put_packs(3, packs)
    send(3)

    arrived(3)
    packs = {}
    for plane in range(lx):
        b = flip(assemble(3, plane))
        a, grad = adjoint([f1[j, plane] for j in range(Q)], b, *blocking(plane))
        grad_out[plane] = grad_out[plane] + grad
        put(4, plane, flip(a), packs)
    put_packs(4, packs)
    send(4)

    arrived(4)
    for plane in range(lx):
        b = flip(assemble(4, plane))
        a, grad = adjoint([f0[j, plane] for j in range(Q)], b, *blocking(plane))
        grad_out[plane] = grad_out[plane] + grad
        for j in range(Q):
            adj_out[j, plane] = a[j]

    for s in range(STREAMS):
        for m in SEND_ORDER:
            copy_of(s, m).wait_send()


def body(sizes, populations, porosity, solid, seed_adjoint):
    lx, ly, lz = porosity.shape
    f32 = jnp.float32
    vmem = functools.partial(pltpu.VMEM, dtype=f32)
    x_shape = (STREAMS, 2, 5, ly, lz)
    y_shape = (STREAMS, 2, 5 * lx, lz)
    z_shape = (STREAMS, 2, ly, lz)
    e1_shape = (STREAMS, 8, 1, lz)
    e2_shape = (STREAMS, 4, lx, lz)
    halo = [
        vmem(shape)
        for shape in (x_shape, y_shape, z_shape, e1_shape, e2_shape)
        for _ in range(2)
    ]
    return pl.pallas_call(
        functools.partial(kernel, sizes),
        out_shape=(
            jax.ShapeDtypeStruct(porosity.shape, f32),
            jax.ShapeDtypeStruct(populations.shape, f32),
        ),
        in_specs=[pl.BlockSpec(memory_space=pl.ANY)] * 4,
        out_specs=(
            pl.BlockSpec(memory_space=pltpu.VMEM),
            pl.BlockSpec(memory_space=pltpu.VMEM),
        ),
        scratch_shapes=[
            vmem(populations.shape),
            vmem(porosity.shape),
            pltpu.VMEM(solid.shape, solid.dtype),
            vmem(populations.shape),
            vmem(populations.shape),
            vmem(populations.shape),
            vmem((STREAMS,) + populations.shape),
            *halo,
            pltpu.SemaphoreType.DMA((4,)),
            pltpu.SemaphoreType.DMA((STREAMS, 18)),
            pltpu.SemaphoreType.DMA((STREAMS, 18)),
        ],
        compiler_params=pltpu.CompilerParams(collective_id=0, has_side_effects=True),
        name="lattice_adjoint",
    )(populations, porosity, solid, seed_adjoint)


def solution(mesh):
    sizes = tuple(mesh.shape[name] for name in AXES)
    cells = P("gx", "gy", "gz")
    field = P(None, "gx", "gy", "gz")
    return jax.shard_map(
        functools.partial(body, sizes),
        mesh=mesh,
        in_specs=(field, cells, cells, field),
        out_specs=(cells, field),
        check_vma=False,
    )
```

```python
import functools

import jax
import jax.numpy as jnp
from jax import lax
from jax.experimental import pallas as pl
from jax.experimental.pallas import tpu as pltpu
from jax.sharding import PartitionSpec as P

STEPS = 3
STREAMS = 5
AXES = ("gx", "gy", "gz")
Q = 19

VEL = [
    (0, 0, 0),
    (1, 0, 0),
    (-1, 0, 0),
    (0, 1, 0),
    (0, -1, 0),
    (0, 0, 1),
    (0, 0, -1),
    (1, 1, 0),
    (-1, -1, 0),
    (1, -1, 0),
    (-1, 1, 0),
    (1, 0, 1),
    (-1, 0, -1),
    (1, 0, -1),
    (-1, 0, 1),
    (0, 1, 1),
    (0, -1, -1),
    (0, 1, -1),
    (0, -1, 1),
]
OPP = [0, 2, 1, 4, 3, 6, 5, 8, 7, 10, 9, 12, 11, 14, 13, 16, 15, 18, 17]
W = [1.0 / 3.0] + [1.0 / 18.0] * 6 + [1.0 / 36.0] * 12
OMEGA = 1.25
PAIRS = [(i, OPP[i]) for i in range(1, Q, 2)]

FACE = {
    m: [j for j in range(Q) if any(c and c == d for c, d in zip(VEL[j], VEL[m]))]
    for m in range(1, 7)
}
SEND_ORDER = [7, 8, 9, 10, 1, 2, 11, 12, 13, 14, 15, 16, 17, 18, 3, 4, 5, 6]


def face_of(axis, sign):
    return 1 + 2 * axis + (0 if sign > 0 else 1)


def signed(terms):
    total = None
    for sign, value in terms:
        if total is None:
            total = value if sign > 0 else -value
        else:
            total = total + value if sign > 0 else total - value
    return total


def moments(odd):
    return [
        signed([(VEL[i][d], odd[i]) for i, _ in PAIRS if VEL[i][d]]) for d in range(3)
    ]


def dot_c(vel, vec):
    return signed([(vel[d], vec[d]) for d in range(3) if vel[d]])


def flow(f):
    even = {i: f[i] + f[o] for i, o in PAIRS}
    odd = {i: f[i] - f[o] for i, o in PAIRS}
    rho = f[0]
    for i, _ in PAIRS:
        rho = rho + even[i]
    inv = 1.0 / rho
    u = [m * inv for m in moments(odd)]
    return even, odd, rho, u


def collide(f, block):
    even, odd, rho, u = flow(f)
    speed = u[0] * u[0] + u[1] * u[1] + u[2] * u[2]
    fluid = 1.0 - block
    keep_even = fluid * (1.0 - OMEGA) + block
    keep_odd = fluid * (1.0 - OMEGA) - block
    push = fluid * OMEGA * rho
    base = 1.0 - 1.5 * speed
    out = [None] * Q
    out[0] = keep_even * f[0] + push * W[0] * base
    half_even = 0.5 * keep_even
    half_odd = 0.5 * keep_odd
    weighted = {w: push * w for w in set(W[1:])}
    for i, o in PAIRS:
        p = dot_c(VEL[i], u)
        scale = weighted[W[i]]
        e = half_even * even[i] + scale * (base + 4.5 * (p * p))
        q = half_odd * odd[i] + scale * (3.0 * p)
        out[i] = e + q
        out[o] = e - q
    return out


def adjoint(f, b, block, open_cell):
    even, odd, rho, u = flow(f)
    speed = u[0] * u[0] + u[1] * u[1] + u[2] * u[2]
    beven = {i: b[i] + b[o] for i, o in PAIRS}
    bodd = {i: b[i] - b[o] for i, o in PAIRS}
    weven = {i: W[i] * beven[i] for i, _ in PAIRS}
    e0 = W[0] * b[0]
    for i, _ in PAIRS:
        e0 = e0 + weven[i]
    e1 = moments({i: W[i] * bodd[i] for i, _ in PAIRS})

    def second(d, k):
        return signed(
            [
                (VEL[i][d] * VEL[i][k], weven[i])
                for i, _ in PAIRS
                if VEL[i][d] * VEL[i][k]
            ]
        )

    q = [[None] * 3 for _ in range(3)]
    for d in range(3):
        for k in range(d, 3):
            q[d][k] = q[k][d] = second(d, k)
    qu = [q[d][0] * u[0] + q[d][1] * u[1] + q[d][2] * u[2] for d in range(3)]
    uqu = qu[0] * u[0] + qu[1] * u[1] + qu[2] * u[2]
    ue1 = e1[0] * u[0] + e1[1] * u[1] + e1[2] * u[2]
    tail = 4.5 * uqu - 1.5 * speed * e0
    b_feq = rho * (e0 + 3.0 * ue1 + tail)
    fluid = 1.0 - block
    push = fluid * OMEGA
    g0 = push * (e0 - tail)
    g = [push * (3.0 * e1[d] + 9.0 * qu[d] - 3.0 * (u[d] * e0)) for d in range(3)]
    se = None
    so = None
    for i, _ in PAIRS:
        x = beven[i] * even[i]
        y = bodd[i] * odd[i]
        se = x if se is None else se + x
        so = y if so is None else so + y
    rest = b[0] * f[0]
    b_f = rest + 0.5 * (se + so)
    b_fopp = rest + 0.5 * (se - so)
    grad = open_cell * (b_fopp - (1.0 - OMEGA) * b_f - OMEGA * b_feq)
    keep_even = fluid * (1.0 - OMEGA) + block
    half_even = 0.5 * keep_even
    half_odd = 0.5 * (fluid * (1.0 - OMEGA) - block)
    a = [None] * Q
    a[0] = keep_even * b[0] + g0
    for i, o in PAIRS:
        e = half_even * beven[i] + g0
        h = half_odd * bodd[i] + dot_c(VEL[i], g)
        a[i] = e + h
        a[o] = e - h
    return a, grad


def kernel(
    sizes,
    f_hbm,
    por_hbm,
    sol_hbm,
    a_hbm,
    grad_out,
    adj_out,
    f0,
    por,
    sol,
    a3,
    f1,
    bbuf,
    post,
    xs,
    xr,
    ys,
    yr,
    zs,
    zr,
    e1s,
    e1r,
    e2s,
    e2r,
    in_sem,
    send_sem,
    recv_sem,
):
    lx, ly, lz = por.shape
    here = [lax.axis_index(name) for name in AXES]

    def neighbour(vel):
        return tuple(
            lax.rem(here[d] + (vel[d] + sizes[d]), sizes[d]) if vel[d] else here[d]
            for d in range(3)
        )

    barrier = pltpu.get_barrier_semaphore()
    for m in SEND_ORDER:
        pl.semaphore_signal(
            barrier,
            inc=1,
            device_id=neighbour(VEL[m]),
            device_id_type=pl.DeviceIdType.MESH,
        )
    loads = [
        pltpu.make_async_copy(src, dst, in_sem.at[k])
        for k, (src, dst) in enumerate(
            [(f_hbm, f0), (por_hbm, por), (sol_hbm, sol), (a_hbm, a3)]
        )
    ]
    for load in loads:
        load.start()

    row = lax.broadcasted_iota(jnp.int32, (ly, lz), 0)
    lane = lax.broadcasted_iota(jnp.int32, (ly, lz), 1)
    lane1 = lax.broadcasted_iota(jnp.int32, (1, lz), 1)
    diagonal = row == lane

    def last(sign, n):
        return n - 1 if sign > 0 else 0

    def buffers(s, m, x, y, z, e1, e2):
        if m <= 2:
            return x.at[s, m - 1]
        if m <= 4:
            return y.at[s, m - 3]
        if m <= 6:
            return z.at[s, m - 5]
        if m <= 14:
            return e1.at[s, m - 7]
        return e2.at[s, m - 15]

    def copy_of(s, m):
        return pltpu.make_async_remote_copy(
            src_ref=buffers(s, m, xs, ys, zs, e1s, e2s),
            dst_ref=buffers(s, m, xr, yr, zr, e1r, e2r),
            send_sem=send_sem.at[s, m - 1],
            recv_sem=recv_sem.at[s, m - 1],
            device_id=neighbour(VEL[m]),
            device_id_type=pl.DeviceIdType.MESH,
        )

    def send(s):
        for m in SEND_ORDER:
            copy_of(s, m).start()

    def arrived(s):
        for m in SEND_ORDER:
            copy_of(s, m).wait_recv()

    def put(s, plane, values, packs):
        for j in range(Q):
            cx, cy, cz = VEL[j]
            v = values[j]
            leaves = cx != 0 and plane == last(cx, lx)
            if leaves:
                m = face_of(0, cx)
                xs[s, m - 1, FACE[m].index(j)] = v
                if cy:
                    r = last(cy, ly)
                    e1s[s, j - 7] = v[r : r + 1, :]
                if cz:
                    c = last(cz, lz)
                    column = jnp.broadcast_to(v[:, c : c + 1], (ly, lz))
                    e1s[s, j - 7] = jnp.sum(
                        jnp.where(diagonal, column, 0.0), axis=0, keepdims=True
                    )
            else:
                post[s, j, plane] = v
            if cy:
                m = face_of(1, cy)
                r = last(cy, ly)
                k = FACE[m].index(j) * lx + plane
                ys[s, m - 3, k : k + 1, :] = v[r : r + 1, :]
                if cz:
                    e2s[s, j - 15, plane : plane + 1, :] = v[r : r + 1, :]
            if cz:
                m = face_of(2, cz)
                k = FACE[m].index(j) * lx + plane
                turned = pltpu.roll(v, (k - last(cz, lz)) % lz, 1)
                old = packs.get(m)
                packs[m] = turned if old is None else jnp.where(lane == k, turned, old)

    def put_packs(s, packs):
        for m in (5, 6):
            zs[s, m - 5] = packs[m]

    def assemble(s, plane):
        packs = [zr[s, 0], zr[s, 1]]
        out = []
        for j in range(Q):
            cx, cy, cz = VEL[j]
            source = plane - cx
            inside = 0 <= source < lx
            if inside:
                v = post[s, j, source]
            else:
                m = face_of(0, cx)
                v = xr[s, m - 1, FACE[m].index(j)]
            if cz:
                c = last(cz, lz)
                if inside:
                    m = face_of(2, cz)
                    k = FACE[m].index(j) * lx + source
                    column = pltpu.roll(packs[m - 5], (c - k) % lz, 1)
                else:
                    line = jnp.broadcast_to(e1r[s, j - 7], (ly, lz))
                    column = jnp.sum(
                        jnp.where(diagonal, line, 0.0), axis=1, keepdims=True
                    )
                v = jnp.where(lane == c, column, v)
            if cy:
                r = last(cy, ly)
                if inside:
                    m = face_of(1, cy)
                    k = FACE[m].index(j) * lx + source
                    line = yr[s, m - 3, k : k + 1, :]
                    if cz:
                        line = jnp.where(
                            lane1 == last(cz, lz),
                            e2r[s, j - 15, source : source + 1, :],
                            line,
                        )
                else:
                    line = e1r[s, j - 7]
                v = jnp.where(row == r, jnp.broadcast_to(line, (ly, lz)), v)
                v = pltpu.roll(v, cy % ly, 0)
            if cz:
                v = pltpu.roll(v, cz % lz, 1)
            out.append(v)
        return out

    def blocking(plane):
        solid = sol[plane] == 1
        return jnp.where(solid, 1.0, por[plane]), jnp.where(solid, 0.0, 1.0)

    def flip(values):
        return [values[OPP[j]] for j in range(Q)]

    for load in loads[:3]:
        load.wait()
    packs = {}
    for plane in range(lx):
        block, _ = blocking(plane)
        put(0, plane, collide([f0[j, plane] for j in range(Q)], block), packs)
    put_packs(0, packs)
    pl.semaphore_wait(barrier, len(SEND_ORDER))
    send(0)

    loads[3].wait()
    packs = {}
    for plane in range(lx):
        put(2, plane, flip([a3[j, plane] for j in range(Q)]), packs)
    put_packs(2, packs)
    send(2)

    arrived(0)
    packs = {}
    for plane in range(lx):
        f = assemble(0, plane)
        for j in range(Q):
            f1[j, plane] = f[j]
        block, _ = blocking(plane)
        put(1, plane, collide(f, block), packs)
    put_packs(1, packs)
    send(1)

    arrived(2)
    for plane in range(lx):
        b = assemble(2, plane)
        for j in range(Q):
            bbuf[j, plane] = b[j]
    arrived(1)
    packs = {}
    for plane in range(lx):
        f = assemble(1, plane)
        b = flip([bbuf[j, plane] for j in range(Q)])
        a, grad = adjoint(f, b, *blocking(plane))
        grad_out[plane] = grad
        put(3, plane, flip(a), packs)
    put_packs(3, packs)
    send(3)

    arrived(3)
    packs = {}
    for plane in range(lx):
        b = flip(assemble(3, plane))
        a, grad = adjoint([f1[j, plane] for j in range(Q)], b, *blocking(plane))
        grad_out[plane] = grad_out[plane] + grad
        put(4, plane, flip(a), packs)
    put_packs(4, packs)
    send(4)

    arrived(4)
    for plane in range(lx):
        b = flip(assemble(4, plane))
        a, grad = adjoint([f0[j, plane] for j in range(Q)], b, *blocking(plane))
        grad_out[plane] = grad_out[plane] + grad
        for j in range(Q):
            adj_out[j, plane] = a[j]

    for s in range(STREAMS):
        for m in SEND_ORDER:
            copy_of(s, m).wait_send()


def write_out(grad, adj, grad_out, adj_out, sem):
    copies = [
        pltpu.make_async_copy(src, dst, sem.at[k])
        for k, (src, dst) in enumerate([(adj, adj_out), (grad, grad_out)])
    ]
    for copy in copies:
        copy.start()
    for copy in copies:
        copy.wait()


def body(sizes, populations, porosity, solid, seed_adjoint):
    lx, ly, lz = porosity.shape
    f32 = jnp.float32
    vmem = functools.partial(pltpu.VMEM, dtype=f32)
    x_shape = (STREAMS, 2, 5, ly, lz)
    y_shape = (STREAMS, 2, 5 * lx, lz)
    z_shape = (STREAMS, 2, ly, lz)
    e1_shape = (STREAMS, 8, 1, lz)
    e2_shape = (STREAMS, 4, lx, lz)
    halo = [
        vmem(shape)
        for shape in (x_shape, y_shape, z_shape, e1_shape, e2_shape)
        for _ in range(2)
    ]
    results = pl.pallas_call(
        functools.partial(kernel, sizes),
        out_shape=(vmem(porosity.shape), vmem(populations.shape)),
        in_specs=[pl.BlockSpec(memory_space=pl.ANY)] * 4,
        out_specs=(
            pl.BlockSpec(memory_space=pltpu.VMEM),
            pl.BlockSpec(memory_space=pltpu.VMEM),
        ),
        scratch_shapes=[
            vmem(populations.shape),
            vmem(porosity.shape),
            pltpu.VMEM(solid.shape, solid.dtype),
            vmem(populations.shape),
            vmem(populations.shape),
            vmem(populations.shape),
            vmem((STREAMS,) + populations.shape),
            *halo,
            pltpu.SemaphoreType.DMA((4,)),
            pltpu.SemaphoreType.DMA((STREAMS, 18)),
            pltpu.SemaphoreType.DMA((STREAMS, 18)),
        ],
        compiler_params=pltpu.CompilerParams(collective_id=0, has_side_effects=True),
        name="lattice_adjoint",
    )(populations, porosity, solid, seed_adjoint)
    return pl.pallas_call(
        write_out,
        out_shape=tuple(jax.ShapeDtypeStruct(r.shape, r.dtype) for r in results),
        in_specs=[pl.BlockSpec(memory_space=pltpu.VMEM)] * 2,
        out_specs=(pl.BlockSpec(memory_space=pl.ANY),) * 2,
        scratch_shapes=[pltpu.SemaphoreType.DMA((2,))],
        name="write_out",
    )(*[pltpu.with_memory_space_constraint(r, pltpu.VMEM) for r in results])


def solution(mesh):
    sizes = tuple(mesh.shape[name] for name in AXES)
    cells = P("gx", "gy", "gz")
    field = P(None, "gx", "gy", "gz")
    return jax.shard_map(
        functools.partial(body, sizes),
        mesh=mesh,
        in_specs=(field, cells, cells, field),
        out_specs=(cells, field),
        check_vma=False,
    )
```

```python
import functools

import jax
import jax.numpy as jnp
from jax import lax
from jax.experimental import pallas as pl
from jax.experimental.pallas import tpu as pltpu
from jax.sharding import PartitionSpec as P

STEPS = 3
STREAMS = 5
AXES = ("gx", "gy", "gz")
Q = 19

VEL = [
    (0, 0, 0),
    (1, 0, 0),
    (-1, 0, 0),
    (0, 1, 0),
    (0, -1, 0),
    (0, 0, 1),
    (0, 0, -1),
    (1, 1, 0),
    (-1, -1, 0),
    (1, -1, 0),
    (-1, 1, 0),
    (1, 0, 1),
    (-1, 0, -1),
    (1, 0, -1),
    (-1, 0, 1),
    (0, 1, 1),
    (0, -1, -1),
    (0, 1, -1),
    (0, -1, 1),
]
OPP = [0, 2, 1, 4, 3, 6, 5, 8, 7, 10, 9, 12, 11, 14, 13, 16, 15, 18, 17]
W = [1.0 / 3.0] + [1.0 / 18.0] * 6 + [1.0 / 36.0] * 12
OMEGA = 1.25
PAIRS = [(i, OPP[i]) for i in range(1, Q, 2)]

FACE = {
    m: [j for j in range(Q) if any(c and c == d for c, d in zip(VEL[j], VEL[m]))]
    for m in range(1, 7)
}
X_MESSAGES = [7, 8, 9, 10, 1, 2, 11, 12, 13, 14]
REST_MESSAGES = [15, 16, 17, 18, 3, 4, 5, 6]
SEND_ORDER = X_MESSAGES + REST_MESSAGES
X_PAIRS = [p for p in PAIRS if VEL[p[0]][0]]
REST_PAIRS = [p for p in PAIRS if not VEL[p[0]][0]]


def face_of(axis, sign):
    return 1 + 2 * axis + (0 if sign > 0 else 1)


def add(total, sign, value):
    if total is None:
        return value if sign > 0 else -value
    return total + value if sign > 0 else total - value


def signed(terms):
    total = None
    for sign, value in terms:
        total = add(total, sign, value)
    return total


def dot_c(vel, vec):
    return signed([(vel[d], vec[d]) for d in range(3) if vel[d]])


class Sums:
    def __init__(self, center, weighted):
        self.center, self.weighted = center, weighted
        self.even, self.odd = {}, {}
        self.total = W[0] * center if weighted else center
        self.first = [None] * 3
        self.second = {}

    def take(self, values, pairs):
        for i, o in pairs:
            even, odd = values[i] + values[o], values[i] - values[o]
            self.even[i], self.odd[i] = even, odd
            if self.weighted:
                even, odd = W[i] * even, W[i] * odd
            self.total = self.total + even
            c = VEL[i]
            for d in range(3):
                if c[d]:
                    self.first[d] = add(self.first[d], c[d], odd)
                if self.weighted:
                    for k in range(d, 3):
                        if c[d] * c[k]:
                            old = self.second.get((d, k))
                            self.second[d, k] = add(old, c[d] * c[k], even)
        return self


class Cells:
    def __init__(self, sums, block):
        self.sums, self.block = sums, block
        self.rho = sums.total
        inv = 1.0 / self.rho
        self.u = [m * inv for m in sums.first]
        u = self.u
        self.speed = u[0] * u[0] + u[1] * u[1] + u[2] * u[2]
        fluid = 1.0 - block
        self.push = fluid * OMEGA
        self.keep_even = fluid * (1.0 - OMEGA) + block
        self.half_even = 0.5 * self.keep_even
        self.half_odd = 0.5 * (fluid * (1.0 - OMEGA) - block)

    def prepare(self):
        push = self.push * self.rho
        self.base = 1.0 - 1.5 * self.speed
        self.weighted = {w: push * w for w in (W[0], W[1], W[7])}

    def collide(self, pairs):
        out = {}
        for i, o in pairs:
            p = dot_c(VEL[i], self.u)
            scale = self.weighted[W[i]]
            e = self.half_even * self.sums.even[i]
            e = e + scale * (self.base + 4.5 * (p * p))
            q = self.half_odd * self.sums.odd[i] + scale * (3.0 * p)
            out[i], out[o] = e + q, e - q
        return out

    def collide_center(self):
        return self.keep_even * self.sums.center + self.weighted[W[0]] * self.base

    def pull(self, b):
        u, e0, e1 = self.u, b.total, b.first
        q = [[b.second[min(d, k), max(d, k)] for k in range(3)] for d in range(3)]
        qu = [q[d][0] * u[0] + q[d][1] * u[1] + q[d][2] * u[2] for d in range(3)]
        uqu = qu[0] * u[0] + qu[1] * u[1] + qu[2] * u[2]
        self.b = b
        self.tail = 4.5 * uqu - 1.5 * self.speed * e0
        self.g0 = self.push * (e0 - self.tail)
        self.g = [
            self.push * (3.0 * e1[d] + 9.0 * qu[d] - 3.0 * (u[d] * e0))
            for d in range(3)
        ]

    def adjoint(self, pairs):
        out = {}
        for i, o in pairs:
            e = self.half_even * self.b.even[i] + self.g0
            h = self.half_odd * self.b.odd[i] + dot_c(VEL[i], self.g)
            out[i], out[o] = e + h, e - h
        return out

    def adjoint_center(self):
        return self.keep_even * self.b.center + self.g0

    def gradient(self, open_cell):
        b, f, u = self.b, self.sums, self.u
        ue1 = b.first[0] * u[0] + b.first[1] * u[1] + b.first[2] * u[2]
        b_feq = self.rho * (b.total + 3.0 * ue1 + self.tail)
        se = signed([(1, b.even[i] * f.even[i]) for i, _ in PAIRS])
        so = signed([(1, b.odd[i] * f.odd[i]) for i, _ in PAIRS])
        rest = b.center * f.center
        b_f = rest + 0.5 * (se + so)
        b_fopp = rest + 0.5 * (se - so)
        return open_cell * (b_fopp - (1.0 - OMEGA) * b_f - OMEGA * b_feq)


def kernel(
    sizes,
    f_hbm,
    por_hbm,
    sol_hbm,
    a_hbm,
    grad_out,
    adj_out,
    f0,
    por,
    sol,
    a3,
    f1,
    post,
    xs,
    xr,
    ys,
    yr,
    zs,
    zr,
    e1s,
    e1r,
    e2s,
    e2r,
    in_sem,
    send_sem,
    recv_sem,
):
    lx, ly, lz = por.shape
    here = [lax.axis_index(name) for name in AXES]

    def neighbour(vel):
        return tuple(
            lax.rem(here[d] + (vel[d] + sizes[d]), sizes[d]) if vel[d] else here[d]
            for d in range(3)
        )

    barrier = pltpu.get_barrier_semaphore()
    for m in SEND_ORDER:
        pl.semaphore_signal(
            barrier,
            inc=1,
            device_id=neighbour(VEL[m]),
            device_id_type=pl.DeviceIdType.MESH,
        )
    loads = [
        pltpu.make_async_copy(src, dst, in_sem.at[k])
        for k, (src, dst) in enumerate(
            [(f_hbm, f0), (por_hbm, por), (sol_hbm, sol), (a_hbm, a3)]
        )
    ]
    for load in loads:
        load.start()

    row = lax.broadcasted_iota(jnp.int32, (ly, lz), 0)
    lane = lax.broadcasted_iota(jnp.int32, (ly, lz), 1)
    lane1 = lax.broadcasted_iota(jnp.int32, (1, lz), 1)
    diagonal = row == lane

    def last(sign, n):
        return n - 1 if sign > 0 else 0

    def buffers(s, m, x, y, z, e1, e2):
        if m <= 2:
            return x.at[s, m - 1]
        if m <= 4:
            return y.at[s, m - 3]
        if m <= 6:
            return z.at[s, m - 5]
        if m <= 14:
            return e1.at[s, m - 7]
        return e2.at[s, m - 15]

    def copy_of(s, m):
        return pltpu.make_async_remote_copy(
            src_ref=buffers(s, m, xs, ys, zs, e1s, e2s),
            dst_ref=buffers(s, m, xr, yr, zr, e1r, e2r),
            send_sem=send_sem.at[s, m - 1],
            recv_sem=recv_sem.at[s, m - 1],
            device_id=neighbour(VEL[m]),
            device_id_type=pl.DeviceIdType.MESH,
        )

    def send(s, messages):
        for m in messages:
            copy_of(s, m).start()

    def arrived(s, messages):
        for m in messages:
            copy_of(s, m).wait_recv()

    def left(s):
        for m in SEND_ORDER:
            copy_of(s, m).wait_send()

    def put_x(s, plane, values):
        for j, v in values.items():
            cx, cy, cz = VEL[j]
            if cx == 0 or plane != last(cx, lx):
                continue
            m = face_of(0, cx)
            xs[s, m - 1, FACE[m].index(j)] = v
            if cy:
                r = last(cy, ly)
                e1s[s, j - 7] = v[r : r + 1, :]
            if cz:
                c = last(cz, lz)
                column = jnp.broadcast_to(v[:, c : c + 1], (ly, lz))
                e1s[s, j - 7] = jnp.sum(
                    jnp.where(diagonal, column, 0.0), axis=0, keepdims=True
                )

    def put_rest(s, plane, values, packs):
        for j, v in values.items():
            cx, cy, cz = VEL[j]
            if cx == 0 or plane != last(cx, lx):
                post[s, j, plane] = v
            if cy:
                m = face_of(1, cy)
                r = last(cy, ly)
                k = FACE[m].index(j) * lx + plane
                ys[s, m - 3, k : k + 1, :] = v[r : r + 1, :]
                if cz:
                    e2s[s, j - 15, plane : plane + 1, :] = v[r : r + 1, :]
            if cz:
                m = face_of(2, cz)
                k = FACE[m].index(j) * lx + plane
                turned = pltpu.roll(v, (k - last(cz, lz)) % lz, 1)
                old = packs.get(m)
                packs[m] = turned if old is None else jnp.where(lane == k, turned, old)

    def put_packs(s, packs):
        for m in (5, 6):
            zs[s, m - 5] = packs[m]

    def assemble(s, plane, late):
        packs = None if late else [zr[s, 0], zr[s, 1]]
        out = {}
        for j in range(Q):
            cx, cy, cz = VEL[j]
            source = plane - cx
            inside = 0 <= source < lx
            if inside == late:
                continue
            if inside:
                v = post[s, j, source]
            else:
                m = face_of(0, cx)
                v = xr[s, m - 1, FACE[m].index(j)]
            if cz:
                c = last(cz, lz)
                if inside:
                    m = face_of(2, cz)
                    k = FACE[m].index(j) * lx + source
                    column = pltpu.roll(packs[m - 5], (c - k) % lz, 1)
                else:
                    line = jnp.broadcast_to(e1r[s, j - 7], (ly, lz))
                    column = jnp.sum(
                        jnp.where(diagonal, line, 0.0), axis=1, keepdims=True
                    )
                v = jnp.where(lane == c, column, v)
            if cy:
                r = last(cy, ly)
                if inside:
                    m = face_of(1, cy)
                    k = FACE[m].index(j) * lx + source
                    line = yr[s, m - 3, k : k + 1, :]
                    if cz:
                        line = jnp.where(
                            lane1 == last(cz, lz),
                            e2r[s, j - 15, source : source + 1, :],
                            line,
                        )
                else:
                    line = e1r[s, j - 7]
                v = jnp.where(row == r, jnp.broadcast_to(line, (ly, lz)), v)
                v = pltpu.roll(v, cy % ly, 0)
            if cz:
                v = pltpu.roll(v, cz % lz, 1)
            out[j] = v
        return out

    def blocking(plane):
        return jnp.where(sol[plane] == 1, 1.0, por[plane])

    def open_cell(plane):
        return jnp.where(sol[plane] == 1, 0.0, 1.0)

    def flip(values):
        return {OPP[j]: v for j, v in values.items()}

    def whole(ref, plane):
        return {j: ref[j, plane] for j in range(Q)}

    planes = range(lx)

    def all_sums(values, weighted):
        return Sums(values[0], weighted).take(values, PAIRS)

    def emit(s, cells, stage):
        out = [stage(c, X_PAIRS) for c in cells]
        for plane in planes:
            put_x(s, plane, out[plane])
        send(s, X_MESSAGES)
        packs = {}
        for plane in planes:
            rest = stage(cells[plane], REST_PAIRS)
            rest[0] = stage(cells[plane], None)
            put_rest(s, plane, {**out[plane], **rest}, packs)
        put_packs(s, packs)
        send(s, REST_MESSAGES)

    def collided(cells, pairs):
        return cells.collide_center() if pairs is None else cells.collide(pairs)

    def pulled(cells, pairs):
        if pairs is None:
            return cells.adjoint_center()
        return flip(cells.adjoint(pairs))

    def receive(s, adjoint, keep=None, after=None):
        turn = flip if adjoint else (lambda values: values)
        arrived(s, REST_MESSAGES)
        values, sums = [], []
        for plane in planes:
            v = turn(assemble(s, plane, False))
            values.append(v)
            sums.append(Sums(v[0], adjoint).take(v, REST_PAIRS))
        if keep is not None:
            for plane in planes:
                for j, v in values[plane].items():
                    keep[j, plane] = v
        if after is not None:
            after()
        arrived(s, X_MESSAGES)
        for plane in planes:
            late = turn(assemble(s, plane, True))
            sums[plane].take({**values[plane], **late}, X_PAIRS)
            values[plane] = late
        return sums, values

    for load in loads[:3]:
        load.wait()
    start = [Cells(all_sums(whole(f0, p), False), blocking(p)) for p in planes]
    out, packs = [], {}
    for c in start:
        c.prepare()
    for plane in planes:
        values = collided(start[plane], PAIRS)
        values[0] = collided(start[plane], None)
        put_x(0, plane, values)
        put_rest(0, plane, values, packs)
    put_packs(0, packs)
    loads[3].wait()
    packs = {}
    for plane in planes:
        values = flip(whole(a3, plane))
        put_x(2, plane, values)
        put_rest(2, plane, values, packs)
    put_packs(2, packs)
    pl.semaphore_wait(barrier, len(SEND_ORDER))
    send(0, SEND_ORDER)
    send(2, SEND_ORDER)

    sums, late = receive(0, False, keep=f1)
    cells = [Cells(sums[p], blocking(p)) for p in planes]
    for c in cells:
        c.prepare()
    emit(1, cells, collided)
    for plane in planes:
        for j, v in late[plane].items():
            f1[j, plane] = v
    left(0)

    b, _ = receive(2, True)
    left(2)
    sums, _ = receive(1, False)
    cells = [Cells(sums[p], blocking(p)) for p in planes]
    for p in planes:
        cells[p].pull(b[p])
    emit(3, cells, pulled)
    for p in planes:
        grad_out[p] = cells[p].gradient(open_cell(p))
    left(1)

    cells = [Cells(all_sums(whole(f1, p), False), blocking(p)) for p in planes]
    b, _ = receive(3, True)
    for p in planes:
        cells[p].pull(b[p])
    emit(4, cells, pulled)
    for p in planes:
        grad_out[p] = grad_out[p] + cells[p].gradient(open_cell(p))
    left(3)

    cells = [Cells(all_sums(whole(f0, p), False), blocking(p)) for p in planes]
    b, _ = receive(4, True, after=lambda: left(4))
    for p in planes:
        cells[p].pull(b[p])
        values = cells[p].adjoint(PAIRS)
        values[0] = cells[p].adjoint_center()
        for j, v in values.items():
            adj_out[j, p] = v
        grad_out[p] = grad_out[p] + cells[p].gradient(open_cell(p))


def write_out(grad, adj, grad_out, adj_out, sem):
    copies = [
        pltpu.make_async_copy(src, dst, sem.at[k])
        for k, (src, dst) in enumerate([(adj, adj_out), (grad, grad_out)])
    ]
    for copy in copies:
        copy.start()
    for copy in copies:
        copy.wait()


def body(sizes, populations, porosity, solid, seed_adjoint):
    lx, ly, lz = porosity.shape
    f32 = jnp.float32
    vmem = functools.partial(pltpu.VMEM, dtype=f32)
    x_shape = (STREAMS, 2, 5, ly, lz)
    y_shape = (STREAMS, 2, 5 * lx, lz)
    z_shape = (STREAMS, 2, ly, lz)
    e1_shape = (STREAMS, 8, 1, lz)
    e2_shape = (STREAMS, 4, lx, lz)
    halo = [
        vmem(shape)
        for shape in (x_shape, y_shape, z_shape, e1_shape, e2_shape)
        for _ in range(2)
    ]
    results = pl.pallas_call(
        functools.partial(kernel, sizes),
        out_shape=(vmem(porosity.shape), vmem(populations.shape)),
        in_specs=[pl.BlockSpec(memory_space=pl.ANY)] * 4,
        out_specs=(
            pl.BlockSpec(memory_space=pltpu.VMEM),
            pl.BlockSpec(memory_space=pltpu.VMEM),
        ),
        scratch_shapes=[
            vmem(populations.shape),
            vmem(porosity.shape),
            pltpu.VMEM(solid.shape, solid.dtype),
            vmem(populations.shape),
            vmem(populations.shape),
            vmem((STREAMS,) + populations.shape),
            *halo,
            pltpu.SemaphoreType.DMA((4,)),
            pltpu.SemaphoreType.DMA((STREAMS, 18)),
            pltpu.SemaphoreType.DMA((STREAMS, 18)),
        ],
        compiler_params=pltpu.CompilerParams(collective_id=0, has_side_effects=True),
        name="lattice_adjoint",
    )(populations, porosity, solid, seed_adjoint)
    return pl.pallas_call(
        write_out,
        out_shape=tuple(jax.ShapeDtypeStruct(r.shape, r.dtype) for r in results),
        in_specs=[pl.BlockSpec(memory_space=pltpu.VMEM)] * 2,
        out_specs=(pl.BlockSpec(memory_space=pl.ANY),) * 2,
        scratch_shapes=[pltpu.SemaphoreType.DMA((2,))],
        name="write_out",
    )(*[pltpu.with_memory_space_constraint(r, pltpu.VMEM) for r in results])


def solution(mesh):
    sizes = tuple(mesh.shape[name] for name in AXES)
    cells = P("gx", "gy", "gz")
    field = P(None, "gx", "gy", "gz")
    return jax.shard_map(
        functools.partial(body, sizes),
        mesh=mesh,
        in_specs=(field, cells, cells, field),
        out_specs=(cells, field),
        check_vma=False,
    )
```

```python
import functools

import jax
import jax.numpy as jnp
from jax import lax
from jax.experimental import pallas as pl
from jax.experimental.pallas import tpu as pltpu
from jax.sharding import PartitionSpec as P

STEPS = 3
STREAMS = 5
AXES = ("gx", "gy", "gz")
Q = 19

VEL = [
    (0, 0, 0),
    (1, 0, 0),
    (-1, 0, 0),
    (0, 1, 0),
    (0, -1, 0),
    (0, 0, 1),
    (0, 0, -1),
    (1, 1, 0),
    (-1, -1, 0),
    (1, -1, 0),
    (-1, 1, 0),
    (1, 0, 1),
    (-1, 0, -1),
    (1, 0, -1),
    (-1, 0, 1),
    (0, 1, 1),
    (0, -1, -1),
    (0, 1, -1),
    (0, -1, 1),
]
OPP = [0, 2, 1, 4, 3, 6, 5, 8, 7, 10, 9, 12, 11, 14, 13, 16, 15, 18, 17]
W = [1.0 / 3.0] + [1.0 / 18.0] * 6 + [1.0 / 36.0] * 12
OMEGA = 1.25
PAIRS = [(i, OPP[i]) for i in range(1, Q, 2)]

FACE = {
    m: [j for j in range(Q) if any(c and c == d for c, d in zip(VEL[j], VEL[m]))]
    for m in range(1, 7)
}
X_MESSAGES = [7, 8, 9, 10, 1, 2, 11, 12, 13, 14]
REST_MESSAGES = [15, 16, 17, 18, 3, 4, 5, 6]
SEND_ORDER = X_MESSAGES + REST_MESSAGES
X_PAIRS = [p for p in PAIRS if VEL[p[0]][0]]
REST_PAIRS = [p for p in PAIRS if not VEL[p[0]][0]]


def face_of(axis, sign):
    return 1 + 2 * axis + (0 if sign > 0 else 1)


def add(total, sign, value):
    if total is None:
        return value if sign > 0 else -value
    return total + value if sign > 0 else total - value


def signed(terms):
    total = None
    for sign, value in terms:
        total = add(total, sign, value)
    return total


def dot_c(vel, vec):
    return signed([(vel[d], vec[d]) for d in range(3) if vel[d]])


class Sums:
    def __init__(self, center, weighted):
        self.center, self.weighted = center, weighted
        self.even, self.odd = {}, {}
        self.total = W[0] * center if weighted else center
        self.first = [None] * 3
        self.second = {}

    def take(self, values, pairs):
        for i, o in pairs:
            even, odd = values[i] + values[o], values[i] - values[o]
            self.even[i], self.odd[i] = even, odd
            if self.weighted:
                even, odd = W[i] * even, W[i] * odd
            self.total = self.total + even
            c = VEL[i]
            for d in range(3):
                if c[d]:
                    self.first[d] = add(self.first[d], c[d], odd)
                if self.weighted:
                    for k in range(d, 3):
                        if c[d] * c[k]:
                            old = self.second.get((d, k))
                            self.second[d, k] = add(old, c[d] * c[k], even)
        return self


class Cells:
    def __init__(self, sums, block):
        self.sums, self.block = sums, block
        self.rho = sums.total
        inv = 1.0 / self.rho
        self.u = [m * inv for m in sums.first]
        u = self.u
        self.speed = u[0] * u[0] + u[1] * u[1] + u[2] * u[2]
        fluid = 1.0 - block
        self.push = fluid * OMEGA
        self.keep_even = fluid * (1.0 - OMEGA) + block
        self.half_even = 0.5 * self.keep_even
        self.half_odd = 0.5 * (fluid * (1.0 - OMEGA) - block)

    def prepare(self):
        push = self.push * self.rho
        self.base = 1.0 - 1.5 * self.speed
        self.weighted = {w: push * w for w in (W[0], W[1], W[7])}

    def collide(self, pairs):
        out = {}
        for i, o in pairs:
            p = dot_c(VEL[i], self.u)
            scale = self.weighted[W[i]]
            e = self.half_even * self.sums.even[i]
            e = e + scale * (self.base + 4.5 * (p * p))
            q = self.half_odd * self.sums.odd[i] + scale * (3.0 * p)
            out[i], out[o] = e + q, e - q
        return out

    def collide_center(self):
        return self.keep_even * self.sums.center + self.weighted[W[0]] * self.base

    def pull(self, b):
        u, e0, e1 = self.u, b.total, b.first
        q = [[b.second[min(d, k), max(d, k)] for k in range(3)] for d in range(3)]
        qu = [q[d][0] * u[0] + q[d][1] * u[1] + q[d][2] * u[2] for d in range(3)]
        uqu = qu[0] * u[0] + qu[1] * u[1] + qu[2] * u[2]
        self.b = b
        self.tail = 4.5 * uqu - 1.5 * self.speed * e0
        self.g0 = self.push * (e0 - self.tail)
        self.g = [
            self.push * (3.0 * e1[d] + 9.0 * qu[d] - 3.0 * (u[d] * e0))
            for d in range(3)
        ]

    def adjoint(self, pairs):
        out = {}
        for i, o in pairs:
            e = self.half_even * self.b.even[i] + self.g0
            h = self.half_odd * self.b.odd[i] + dot_c(VEL[i], self.g)
            out[i], out[o] = e + h, e - h
        return out

    def adjoint_center(self):
        return self.keep_even * self.b.center + self.g0

    def gradient(self, open_cell):
        b, f, u = self.b, self.sums, self.u
        ue1 = b.first[0] * u[0] + b.first[1] * u[1] + b.first[2] * u[2]
        b_feq = self.rho * (b.total + 3.0 * ue1 + self.tail)
        se = signed([(1, b.even[i] * f.even[i]) for i, _ in PAIRS])
        so = signed([(1, b.odd[i] * f.odd[i]) for i, _ in PAIRS])
        rest = b.center * f.center
        b_f = rest + 0.5 * (se + so)
        b_fopp = rest + 0.5 * (se - so)
        return open_cell * (b_fopp - (1.0 - OMEGA) * b_f - OMEGA * b_feq)


def kernel(
    sizes,
    f_hbm,
    por_hbm,
    sol_hbm,
    a_hbm,
    grad_out,
    adj_out,
    f0,
    por,
    sol,
    a3,
    f1,
    post,
    xs,
    xr,
    ys,
    yr,
    zs,
    zr,
    e1s,
    e1r,
    e2s,
    e2r,
    in_sem,
    send_sem,
    recv_sem,
):
    lx, ly, lz = por.shape
    here = [lax.axis_index(name) for name in AXES]

    def neighbour(vel):
        return tuple(
            lax.rem(here[d] + (vel[d] + sizes[d]), sizes[d]) if vel[d] else here[d]
            for d in range(3)
        )

    barrier = pltpu.get_barrier_semaphore()
    for m in SEND_ORDER:
        pl.semaphore_signal(
            barrier,
            inc=1,
            device_id=neighbour(VEL[m]),
            device_id_type=pl.DeviceIdType.MESH,
        )
    loads = [
        pltpu.make_async_copy(src, dst, in_sem.at[k])
        for k, (src, dst) in enumerate(
            [(f_hbm, f0), (por_hbm, por), (sol_hbm, sol), (a_hbm, a3)]
        )
    ]
    for load in loads:
        load.start()

    row = lax.broadcasted_iota(jnp.int32, (ly, lz), 0)
    lane = lax.broadcasted_iota(jnp.int32, (ly, lz), 1)
    lane1 = lax.broadcasted_iota(jnp.int32, (1, lz), 1)
    diagonal = row == lane

    def last(sign, n):
        return n - 1 if sign > 0 else 0

    def buffers(s, m, x, y, z, e1, e2):
        if m <= 2:
            return x.at[s, m - 1]
        if m <= 4:
            return y.at[s, m - 3]
        if m <= 6:
            return z.at[s, m - 5]
        if m <= 14:
            return e1.at[s, m - 7]
        return e2.at[s, m - 15]

    def copy_of(s, m):
        return pltpu.make_async_remote_copy(
            src_ref=buffers(s, m, xs, ys, zs, e1s, e2s),
            dst_ref=buffers(s, m, xr, yr, zr, e1r, e2r),
            send_sem=send_sem.at[s, m - 1],
            recv_sem=recv_sem.at[s, m - 1],
            device_id=neighbour(VEL[m]),
            device_id_type=pl.DeviceIdType.MESH,
        )

    def send(s, messages):
        for m in messages:
            copy_of(s, m).start()

    def arrived(s, messages):
        for m in messages:
            copy_of(s, m).wait_recv()

    def left(s):
        for m in SEND_ORDER:
            copy_of(s, m).wait_send()

    def put_x(s, plane, values):
        for j, v in values.items():
            cx, cy, cz = VEL[j]
            if cx == 0 or plane != last(cx, lx):
                continue
            m = face_of(0, cx)
            xs[s, m - 1, FACE[m].index(j)] = v
            if cy:
                r = last(cy, ly)
                e1s[s, j - 7] = v[r : r + 1, :]
            if cz:
                c = last(cz, lz)
                column = jnp.broadcast_to(v[:, c : c + 1], (ly, lz))
                e1s[s, j - 7] = jnp.sum(
                    jnp.where(diagonal, column, 0.0), axis=0, keepdims=True
                )

    def put_rest(s, plane, values, packs):
        for j, v in values.items():
            cx, cy, cz = VEL[j]
            if cx == 0 or plane != last(cx, lx):
                post[s, j, plane] = v
            if cy:
                m = face_of(1, cy)
                r = last(cy, ly)
                k = FACE[m].index(j) * lx + plane
                ys[s, m - 3, k : k + 1, :] = v[r : r + 1, :]
                if cz:
                    e2s[s, j - 15, plane : plane + 1, :] = v[r : r + 1, :]
            if cz:
                m = face_of(2, cz)
                k = FACE[m].index(j) * lx + plane
                turned = pltpu.roll(v, (k - last(cz, lz)) % lz, 1)
                old = packs.get(m)
                packs[m] = turned if old is None else jnp.where(lane == k, turned, old)

    def put_packs(s, packs):
        for m in (5, 6):
            zs[s, m - 5] = packs[m]

    def assemble(s, plane, late):
        packs = None if late else [zr[s, 0], zr[s, 1]]
        out = {}
        for j in range(Q):
            cx, cy, cz = VEL[j]
            source = plane - cx
            inside = 0 <= source < lx
            if inside == late:
                continue
            if inside:
                v = post[s, j, source]
            else:
                m = face_of(0, cx)
                v = xr[s, m - 1, FACE[m].index(j)]
            if cz:
                c = last(cz, lz)
                if inside:
                    m = face_of(2, cz)
                    k = FACE[m].index(j) * lx + source
                    column = pltpu.roll(packs[m - 5], (c - k) % lz, 1)
                else:
                    line = jnp.broadcast_to(e1r[s, j - 7], (ly, lz))
                    column = jnp.sum(
                        jnp.where(diagonal, line, 0.0), axis=1, keepdims=True
                    )
                v = jnp.where(lane == c, column, v)
            if cy:
                r = last(cy, ly)
                if inside:
                    m = face_of(1, cy)
                    k = FACE[m].index(j) * lx + source
                    line = yr[s, m - 3, k : k + 1, :]
                    if cz:
                        line = jnp.where(
                            lane1 == last(cz, lz),
                            e2r[s, j - 15, source : source + 1, :],
                            line,
                        )
                else:
                    line = e1r[s, j - 7]
                v = jnp.where(row == r, jnp.broadcast_to(line, (ly, lz)), v)
                v = pltpu.roll(v, cy % ly, 0)
            if cz:
                v = pltpu.roll(v, cz % lz, 1)
            out[j] = v
        return out

    def blocking(plane):
        return jnp.where(sol[plane] == 1, 1.0, por[plane])

    def open_cell(plane):
        return jnp.where(sol[plane] == 1, 0.0, 1.0)

    def flip(values):
        return {OPP[j]: v for j, v in values.items()}

    def whole(ref, plane):
        return {j: ref[j, plane] for j in range(Q)}

    planes = range(lx)

    def all_sums(values, weighted):
        return Sums(values[0], weighted).take(values, PAIRS)

    def emit(s, cells, stage):
        out = {}
        for sign in (1, -1):
            plane = last(sign, lx)
            if plane not in out:
                out[plane] = stage(cells[plane], X_PAIRS)
            going = {j: v for j, v in out[plane].items() if VEL[j][0] == sign}
            put_x(s, plane, going)
            send(s, [m for m in X_MESSAGES if VEL[m][0] == sign])
        for plane in planes:
            if plane not in out:
                out[plane] = stage(cells[plane], X_PAIRS)
        packs = {}
        for plane in planes:
            rest = stage(cells[plane], REST_PAIRS)
            rest[0] = stage(cells[plane], None)
            put_rest(s, plane, {**out[plane], **rest}, packs)
        put_packs(s, packs)
        send(s, REST_MESSAGES)

    def collided(cells, pairs):
        return cells.collide_center() if pairs is None else cells.collide(pairs)

    def pulled(cells, pairs):
        if pairs is None:
            return cells.adjoint_center()
        return flip(cells.adjoint(pairs))

    def receive(s, adjoint, keep=None, after=None):
        turn = flip if adjoint else (lambda values: values)
        arrived(s, REST_MESSAGES)
        values, sums = [], []
        for plane in planes:
            v = turn(assemble(s, plane, False))
            values.append(v)
            sums.append(Sums(v[0], adjoint).take(v, REST_PAIRS))
        if keep is not None:
            for plane in planes:
                for j, v in values[plane].items():
                    keep[j, plane] = v
        if after is not None:
            after()
        arrived(s, X_MESSAGES)
        for plane in planes:
            late = turn(assemble(s, plane, True))
            sums[plane].take({**values[plane], **late}, X_PAIRS)
            values[plane] = late
        return sums, values

    for load in loads[:3]:
        load.wait()
    start = [Cells(all_sums(whole(f0, p), False), blocking(p)) for p in planes]
    out, packs = [], {}
    for c in start:
        c.prepare()
    for plane in planes:
        values = collided(start[plane], PAIRS)
        values[0] = collided(start[plane], None)
        put_x(0, plane, values)
        put_rest(0, plane, values, packs)
    put_packs(0, packs)
    loads[3].wait()
    packs = {}
    for plane in planes:
        values = flip(whole(a3, plane))
        put_x(2, plane, values)
        put_rest(2, plane, values, packs)
    put_packs(2, packs)
    pl.semaphore_wait(barrier, len(SEND_ORDER))
    send(0, SEND_ORDER)
    send(2, SEND_ORDER)

    sums, late = receive(0, False, keep=f1)
    cells = [Cells(sums[p], blocking(p)) for p in planes]
    for c in cells:
        c.prepare()
    emit(1, cells, collided)
    for plane in planes:
        for j, v in late[plane].items():
            f1[j, plane] = v
    left(0)

    b, _ = receive(2, True)
    left(2)
    sums, _ = receive(1, False)
    cells = [Cells(sums[p], blocking(p)) for p in planes]
    for p in planes:
        cells[p].pull(b[p])
    emit(3, cells, pulled)
    for p in planes:
        grad_out[p] = cells[p].gradient(open_cell(p))
    left(1)

    cells = [Cells(all_sums(whole(f1, p), False), blocking(p)) for p in planes]
    b, _ = receive(3, True)
    for p in planes:
        cells[p].pull(b[p])
    emit(4, cells, pulled)
    for p in planes:
        grad_out[p] = grad_out[p] + cells[p].gradient(open_cell(p))
    left(3)

    cells = [Cells(all_sums(whole(f0, p), False), blocking(p)) for p in planes]
    b, _ = receive(4, True, after=lambda: left(4))
    for p in planes:
        cells[p].pull(b[p])
        values = cells[p].adjoint(PAIRS)
        values[0] = cells[p].adjoint_center()
        for j, v in values.items():
            adj_out[j, p] = v
        grad_out[p] = grad_out[p] + cells[p].gradient(open_cell(p))


def write_out(grad, adj, grad_out, adj_out, sem):
    copies = [
        pltpu.make_async_copy(src, dst, sem.at[k])
        for k, (src, dst) in enumerate([(adj, adj_out), (grad, grad_out)])
    ]
    for copy in copies:
        copy.start()
    for copy in copies:
        copy.wait()


def body(sizes, populations, porosity, solid, seed_adjoint):
    lx, ly, lz = porosity.shape
    f32 = jnp.float32
    vmem = functools.partial(pltpu.VMEM, dtype=f32)
    x_shape = (STREAMS, 2, 5, ly, lz)
    y_shape = (STREAMS, 2, 5 * lx, lz)
    z_shape = (STREAMS, 2, ly, lz)
    e1_shape = (STREAMS, 8, 1, lz)
    e2_shape = (STREAMS, 4, lx, lz)
    halo = [
        vmem(shape)
        for shape in (x_shape, y_shape, z_shape, e1_shape, e2_shape)
        for _ in range(2)
    ]
    results = pl.pallas_call(
        functools.partial(kernel, sizes),
        out_shape=(vmem(porosity.shape), vmem(populations.shape)),
        in_specs=[pl.BlockSpec(memory_space=pl.ANY)] * 4,
        out_specs=(
            pl.BlockSpec(memory_space=pltpu.VMEM),
            pl.BlockSpec(memory_space=pltpu.VMEM),
        ),
        scratch_shapes=[
            vmem(populations.shape),
            vmem(porosity.shape),
            pltpu.VMEM(solid.shape, solid.dtype),
            vmem(populations.shape),
            vmem(populations.shape),
            vmem((STREAMS,) + populations.shape),
            *halo,
            pltpu.SemaphoreType.DMA((4,)),
            pltpu.SemaphoreType.DMA((STREAMS, 18)),
            pltpu.SemaphoreType.DMA((STREAMS, 18)),
        ],
        compiler_params=pltpu.CompilerParams(collective_id=0, has_side_effects=True),
        name="lattice_adjoint",
    )(populations, porosity, solid, seed_adjoint)
    return pl.pallas_call(
        write_out,
        out_shape=tuple(jax.ShapeDtypeStruct(r.shape, r.dtype) for r in results),
        in_specs=[pl.BlockSpec(memory_space=pltpu.VMEM)] * 2,
        out_specs=(pl.BlockSpec(memory_space=pl.ANY),) * 2,
        scratch_shapes=[pltpu.SemaphoreType.DMA((2,))],
        name="write_out",
    )(*[pltpu.with_memory_space_constraint(r, pltpu.VMEM) for r in results])


def solution(mesh):
    sizes = tuple(mesh.shape[name] for name in AXES)
    cells = P("gx", "gy", "gz")
    field = P(None, "gx", "gy", "gz")
    return jax.shard_map(
        functools.partial(body, sizes),
        mesh=mesh,
        in_specs=(field, cells, cells, field),
        out_specs=(cells, field),
        check_vma=False,
    )
```
